256 devices in a mesh: rows: 64 (over z, x, core), feat: 4 (over y).
Axes of the slice: x: 4, y: 4, z: 8, core: 2. Of those that a mesh axis runs over, the one named last changes fastest.
Arguments:
- predictions: bfloat16 [98304, 4096], P('rows', 'feat'), may hold values from -6 to 6
- labels: bfloat16 [98304, 4096], P('rows', 'feat'), may hold values from 0 to 1
- feature_codes: int32 [32, 98304], P('feat', 'rows'), may hold values from 0 to 255
- leaf_index: int32 [98304], P('rows'), may hold values from 0 to 63
- sketch_weight: bfloat16 [4096, 256], P('feat'), may hold values from -0.09375 to 0.09375
Outputs:
- histograms: float32 [256, 32, 256], P('rows', 'feat')
- leaf_values: float32 [64, 4096], P(None, 'feat')
- updated: bfloat16 [98304, 4096], P('rows', 'feat')
The draws below stay inside these ranges and needn't reach their ends.
All inputs are finite; a program needn't handle non-finite values.
Results may differ from the reference program's by a relative error of at most 0.008.
Values may be sent and summed in bfloat16 or wider, within the bound.
A program may use at most 64 MiB of HBM per device.

```python
import jax
import jax.numpy as jnp
from jax import lax

LABELS = 4096
SKETCH = 256
BINS = 256
LEAVES = 64
ROW_DEV = 1536
ROWS = 98304
FEATURES = 32
N_FEAT = 4


def shared_leaves(key):
    return jax.random.randint(jax.random.fold_in(key, 101), (ROWS,), 0, LEAVES).astype(jnp.int32)


def label_blocks():
    return jnp.arange(LABELS, dtype=jnp.int32) // 16


def draw_leaf_index(key, part):
    return shared_leaves(key)


def draw_predictions(key, part):
    leaves = shared_leaves(key)
    block_count = (LABELS + 15) // 16
    table = jax.random.uniform(jax.random.fold_in(key, 202), (LEAVES, block_count), jnp.float32, -0.8, 0.8)
    factor_rows = jnp.exp(table)[leaves]
    factor = factor_rows[:, label_blocks()]
    noise_key = jax.random.fold_in(key, 203)
    base = jnp.clip(1.5 * jax.random.normal(noise_key, (ROWS, LABELS), jnp.float32), -5.0, 5.0)
    return jnp.clip(base * factor, -6.0, 6.0).astype(jnp.bfloat16)


def draw_labels(key, part):
    leaves = shared_leaves(key)
    block_count = (LABELS + 15) // 16
    centre = jax.random.uniform(jax.random.fold_in(key, 303), (LEAVES, block_count), jnp.float32, 0.15, 0.85)
    centre_full = centre[leaves][:, label_blocks()]
    noise_key = jax.random.fold_in(key, 304)
    noise = jax.random.uniform(noise_key, (ROWS, LABELS), jnp.float32, -0.15, 0.15)
    return jnp.clip(centre_full + noise, 0.0, 1.0).astype(jnp.bfloat16)


def plant(drawn, own_key, least, largest):
    longest = drawn.shape.index(max(drawn.shape))
    spots = []
    for shift in (0, 1):
        where = [jax.random.randint(jax.random.fold_in(own_key, axis), (), 0, length) for axis, length in enumerate(drawn.shape)]
        where[longest] = (where[longest] + shift) % drawn.shape[longest]
        spots.append(tuple(where))
    return drawn.at[spots[0]].set(least).at[spots[1]].set(largest)


def level_of(key, extent, cuts, low, largest):
    loudness = 1.0
    for axis_at, parts in cuts:
        heights = jax.random.uniform(jax.random.fold_in(jax.random.fold_in(key, 6), axis_at), (parts,), jnp.float32, low / len(cuts), largest / len(cuts))
        loudness = loudness * jnp.repeat(jnp.exp(heights), extent[axis_at] // parts).reshape((-1,) + (1,) * (len(extent) - 1 - axis_at))
    return loudness


def centred(rng, shape, spread, limit, shards=(), kind=jnp.bfloat16):
    gain = level_of(rng, shape, shards, -0.22, 0.18) if shards else 1.0
    array = jax.random.normal(rng, shape, jnp.float32) * spread * gain
    return jnp.minimum(jnp.maximum(array, -limit), limit).astype(kind)


def setup_inputs(seed: int = 0) -> dict:
    key_list = jax.random.split(jax.random.key(seed), 6)
    return {
        "predictions": draw_predictions(jax.random.fold_in(key_list[5], 71), 0),
        "labels": draw_labels(jax.random.fold_in(key_list[5], 71), 0),
        "feature_codes": plant(jax.random.randint(key_list[2], (FEATURES, ROWS), 0, BINS), jax.random.fold_in(key_list[2], 1), 0, BINS - 1).astype(jnp.int32),
        "leaf_index": draw_leaf_index(jax.random.fold_in(key_list[5], 71), 0),
        "sketch_weight": centred(key_list[4], (LABELS, SKETCH), LABELS ** -0.5, 0.09375, ((0, 4),)),
    }


shrinkage = 0.5
ridge_term = 1.0


def reference(predictions, labels, feature_codes, leaf_index, sketch_weight):
    blocks = predictions.shape[0] // ROW_DEV
    features = feature_codes.shape[0]
    width = predictions.shape[1]
    group_width = width // N_FEAT

    def one_block(carry, number):
        hist_acc, grad_acc, hess_acc = carry
        first = (number * ROW_DEV).astype(jnp.int32)
        logits = lax.dynamic_slice_in_dim(predictions, first, ROW_DEV, 0).astype(jnp.float32)
        targets = lax.dynamic_slice_in_dim(labels, first, ROW_DEV, 0).astype(jnp.float32)
        codes = lax.dynamic_slice_in_dim(feature_codes, first, ROW_DEV, 1)
        leaves = lax.dynamic_slice_in_dim(leaf_index, first, ROW_DEV, 0)
        probability = jax.nn.sigmoid(logits)
        gradient = (targets - probability).astype(jnp.bfloat16)
        hessian = (probability * (1.0 - probability)).astype(jnp.bfloat16)
        summed = jnp.zeros((ROW_DEV, SKETCH), jnp.float32)
        for group in range(N_FEAT):
            part = jnp.dot(gradient[:, group * group_width:(group + 1) * group_width],
                           sketch_weight[group * group_width:(group + 1) * group_width, :],
                           preferred_element_type=jnp.float32).astype(jnp.bfloat16)
            summed = summed + part.astype(jnp.float32)
        sketch = summed.astype(jnp.bfloat16)
        levels = jnp.arange(BINS, dtype=jnp.int32)
        one_hot = (levels[:, None, None] == codes[None, :, :]).astype(jnp.float32)
        hist_acc = hist_acc + jnp.einsum("bfr,rk->bfk", one_hot, sketch.astype(jnp.float32))
        leaf_hot = (jnp.arange(LEAVES, dtype=jnp.int32)[:, None] == leaves[None, :]).astype(jnp.bfloat16)
        grad_acc = grad_acc + jnp.dot(leaf_hot, gradient, preferred_element_type=jnp.float32)
        hess_acc = hess_acc + jnp.dot(leaf_hot, hessian, preferred_element_type=jnp.float32)
        return (hist_acc, grad_acc, hess_acc), None

    start_carry = (jnp.zeros((BINS, features, SKETCH), jnp.float32),
                   jnp.zeros((LEAVES, width), jnp.float32),
                   jnp.zeros((LEAVES, width), jnp.float32))
    (histograms, grad_sum, hess_sum), _ = lax.scan(one_block, start_carry, jnp.arange(blocks, dtype=jnp.int32))
    leaf_values = grad_sum / (hess_sum + ridge_term)

    def update_block(pieces):
        logits, leaves = pieces
        return (logits.astype(jnp.float32) + shrinkage * leaf_values[leaves]).astype(jnp.bfloat16)

    shaped = predictions.reshape(blocks, ROW_DEV, width)
    shaped_leaves = leaf_index.reshape(blocks, ROW_DEV)
    updated = lax.map(update_block, (shaped, shaped_leaves)).reshape(blocks * ROW_DEV, width)
    return histograms, leaf_values, updated
```

```python
import jax
import jax.numpy as jnp
from jax import lax
from jax.experimental import pallas as pl
from jax.experimental.pallas import tpu as pltpu
from jax.sharding import PartitionSpec as P

BINS = 256
LEAVES = 64
NZ, NX, NC, NY = 8, 4, 2, 4
R, L, K, F = 1536, 1024, 256, 8
Q = R // NY
H = Q // 2
OWN = BINS // LEAVES * F
PIECE = NZ * OWN
MESH = pl.DeviceIdType.MESH
F32, BF16 = jnp.float32, jnp.bfloat16

shrinkage = 0.5
ridge_term = 1.0

RS, AG, LC, LX, LZ, VX, VC, HC, HX, HZ = 0, 6, 12, 13, 16, 23, 26, 27, 31, 37
COPIES = 44


def owner(slot):
    return (slot & 7) * 8 + ((slot >> 3) & 3) * 2 + (slot >> 5)


def kernel(pred_hbm, lab_hbm, codes_hbm, leaf_hbm, w_hbm,
           hist_ref, value_ref, upd_ref,
           pred, lab, codes, leaf, w, grad, hess, part, rs1, rs2, rsum, sk, hot, oh,
           lsum, lcs, lcr, lxs, lxr, lz, lv, acc, hcs, hcr, hxs, hx1, hx2, hxsum, hzs, hzr,
           load_sem, send, recv):
    row = lax.axis_index("rows")
    y = lax.axis_index("feat")
    c = lax.rem(row, NC)
    x = lax.rem(row // NC, NX)
    z = row // (NC * NX)

    def at(zz, xx, cc):
        return (zz * NX + xx) * NC + cc

    def step(v, d, n):
        return lax.rem(v + d, n)

    partner = (at(z, x, 1 - c), y)
    ypeer = [(row, step(y, d, NY)) for d in range(NY)]
    xpeer = [(at(z, step(x, d, NX), c), y) for d in range(NX)]
    zpeer = [(at(step(z, d, NZ), x, c), y) for d in range(NZ)]

    def copy(n, src, dst, to):
        return pltpu.make_async_remote_copy(
            src_ref=src, dst_ref=dst, send_sem=send.at[n], recv_sem=recv.at[n],
            device_id=to, device_id_type=MESH)

    barrier = pltpu.get_barrier_semaphore()
    peers = [partner] + ypeer[1::2] + xpeer[1:] + zpeer[1:]
    for peer in peers:
        pl.semaphore_signal(barrier, inc=1, device_id=peer, device_id_type=MESH)

    order = [step(y, 2, NY), step(y, 1, NY), step(y, 3, NY), y]
    loads = []
    for i, q in enumerate(order):
        rows = pl.ds(pl.multiple_of(q * Q, Q), Q)
        loads.append((
            pltpu.make_async_copy(pred_hbm.at[rows], pred.at[q], load_sem.at[2 * i]),
            pltpu.make_async_copy(lab_hbm.at[rows], lab.at[q], load_sem.at[2 * i + 1]),
        ))
    small = [
        pltpu.make_async_copy(leaf_hbm, leaf, load_sem.at[8]),
        pltpu.make_async_copy(w_hbm, w, load_sem.at[9]),
        pltpu.make_async_copy(codes_hbm, codes, load_sem.at[10]),
    ]
    small[0].start()
    for cp in loads[0]:
        cp.start()
    small[1].start()
    for cp in loads[1] + loads[2] + loads[3]:
        cp.start()
    small[2].start()
    small[0].wait()

    slots = lax.broadcasted_iota(jnp.int32, (LEAVES, Q), 0)
    lane_owner = owner(slots)
    for q in range(NY):
        here = leaf[:, q * Q:(q + 1) * Q] == lane_owner
        hot[q] = jnp.where(here, 1.0, 0.0).astype(BF16)

    def block(i):
        q = order[i]
        for cp in loads[i]:
            cp.wait()

        def rows16(j, carry):
            rows = pl.ds(pl.multiple_of(j * 16, 16), 16)
            logits = pred[q, rows, :].astype(F32)
            probability = 0.5 + 0.5 * jnp.tanh(0.5 * logits)
            grad[rows, :] = (lab[q, rows, :].astype(F32) - probability).astype(BF16)
            hess[rows, :] = (probability * (1.0 - probability)).astype(BF16)
            return carry

        lax.fori_loop(0, Q // 16, rows16, 0)
        if i == 0:
            small[1].wait()
        part[q] = jnp.dot(grad[...], w[...], preferred_element_type=F32).astype(BF16)

    def leaf_sums(i):
        q = order[i]
        for n, src in ((0, grad), (1, hess)):
            cols = pl.ds(n * L, L)
            s = jnp.dot(hot[q], src[...], preferred_element_type=F32)
            lsum[:, cols] = s if i == 0 else lsum[:, cols] + s

    top, low = pl.ds(0, H), pl.ds(H, H)
    q2, q1, q3, q0 = order
    rs = [
        copy(RS + 0, part.at[q2, top], rs1.at[0], ypeer[1]),
        copy(RS + 1, part.at[q2, low], rs1.at[1], ypeer[3]),
        copy(RS + 2, part.at[q1, low], rs2.at[0, 1], ypeer[1]),
        copy(RS + 3, part.at[q3, top], rs2.at[1, 0], ypeer[3]),
        copy(RS + 4, rsum.at[0], rs2.at[0, 0], ypeer[1]),
        copy(RS + 5, rsum.at[1], rs2.at[1, 1], ypeer[3]),
    ]
    block(0)
    pl.semaphore_wait(barrier, len(peers))
    rs[0].start()
    rs[1].start()
    leaf_sums(0)
    block(1)
    rs[2].start()
    leaf_sums(1)
    block(2)
    rs[3].start()
    leaf_sums(2)
    rs[0].wait_recv()
    rsum[0] = (part[q1, top, :].astype(F32) + rs1[0].astype(F32)).astype(BF16)
    rs[4].start()
    rs[1].wait_recv()
    rsum[1] = (part[q3, low, :].astype(F32) + rs1[1].astype(F32)).astype(BF16)
    rs[5].start()
    block(3)
    leaf_sums(3)

    give, keep = pl.ds((1 - c) * 32, 32), pl.ds(c * 32, 32)
    given = lsum[pl.ds(pl.multiple_of((1 - c) * 32, 32), 32), :].astype(BF16)
    for i in range(NX):
        lcs[i] = given[i * 8:(i + 1) * 8, :]
    lc = copy(LC, lcs, lcr, partner)
    lc.start()

    small[2].wait()
    offset = jnp.where(lax.broadcasted_iota(jnp.int32, (16, R), 0) >= 8, 1, 0)
    pair = (jnp.concatenate([codes[...], codes[...]], axis=0) - offset).astype(BF16)

    def bins_of(s, carry):
        first = owner(s) * 4
        for b in (0, 2):
            level = jnp.full((16, R), first + b, jnp.int32).astype(BF16)
            ones = jnp.where(pair == level, jnp.ones((), BF16), jnp.zeros((), BF16))
            rows = pl.ds(pl.multiple_of(s * 32 + b * 8, 16), 16)
            for q in range(NY):
                oh[q, rows, :] = ones[:, q * Q:(q + 1) * Q]
        return carry

    lax.fori_loop(0, LEAVES, bins_of, 0)

    rs[3].wait_recv()
    rs[4].wait_recv()
    own = part[q0, top, :].astype(F32) + rs2[0, 0].astype(F32) + rs2[1, 0].astype(F32)
    sk[q0, top, :] = own.astype(BF16)
    ag = [
        copy(AG + 0, sk.at[q0, top], sk.at[q0, top], ypeer[1]),
        copy(AG + 1, sk.at[q0, low], sk.at[q0, low], ypeer[3]),
        copy(AG + 2, sk.at[q0, low], sk.at[q0, low], ypeer[1]),
        copy(AG + 3, sk.at[q0, top], sk.at[q0, top], ypeer[3]),
        copy(AG + 4, sk.at[q3, top], sk.at[q3, top], ypeer[1]),
        copy(AG + 5, sk.at[q1, low], sk.at[q1, low], ypeer[3]),
    ]

    def arrival(n, dst):
        copy(n, dst, dst, partner).wait_recv()

    ag[0].start()
    rs[2].wait_recv()
    rs[5].wait_recv()
    own = part[q0, low, :].astype(F32) + rs2[0, 1].astype(F32) + rs2[1, 1].astype(F32)
    sk[q0, low, :] = own.astype(BF16)
    ag[1].start()
    ag[2].start()
    ag[3].start()

    lc.wait_recv()
    kept = lsum[pl.ds(pl.multiple_of(c * 32, 32), 32), :]
    for i in range(NX):
        lsum[pl.ds(i * 8, 8), :] = kept[i * 8:(i + 1) * 8, :] + lcr[i].astype(F32)
    lx = []
    for d in (2, 1, 3):
        to = step(x, d, NX)
        lxs[d - 1] = lsum[pl.ds(pl.multiple_of(to * 8, 8), 8), :].astype(BF16)
        lx.append(copy(LX + d - 1, lxs.at[d - 1], lxr.at[d - 1], xpeer[d]))
        lx[-1].start()

    def add_hist(q, m, first):
        rows = pl.ds(pl.multiple_of(m * PIECE, PIECE), PIECE)
        s = jnp.dot(oh[q, rows, :], sk[q], preferred_element_type=F32)
        return s if first else acc[rows, :] + s

    def hist_of(q, first=False):
        def body(m, carry):
            rows = pl.ds(pl.multiple_of(m * PIECE, PIECE), PIECE)
            acc[rows, :] = add_hist(q, m, first)
            return carry

        lax.fori_loop(0, NC * NX, body, 0)

    hist_of(q0, True)

    for cp in lx:
        cp.wait_recv()
    mine = lsum[pl.ds(pl.multiple_of(x * 8, 8), 8), :]
    for d in range(3):
        mine = mine + lxr[d].astype(F32)
    lz[z] = mine.astype(BF16)
    lzc = [copy(LZ + d - 1, lz.at[z], lz.at[z], zpeer[d]) for d in (4, 3, 5, 2, 6, 1, 7)]
    for cp in lzc:
        cp.start()

    arrival(AG + 0, sk.at[q3, top])
    ag[4].start()
    arrival(AG + 1, sk.at[q1, low])
    ag[5].start()
    arrival(AG + 2, sk.at[q3, low])
    hist_of(q3)
    arrival(AG + 3, sk.at[q1, top])
    hist_of(q1)
    arrival(AG + 4, sk.at[q2, top])
    arrival(AG + 5, sk.at[q2, low])

    xorder = [step(x, 2, NX), step(x, 1, NX), step(x, 3, NX), x]
    hc = []
    for i, to in enumerate(xorder):
        hcs[to] = add_hist(q2, (1 - c) * NX + to, False).astype(BF16)
        hc.append(copy(HC + i, hcs.at[to], hcr.at[to], partner))
        hc[-1].start()
    for to in xorder:
        acc[pl.ds(pl.multiple_of(to * PIECE, PIECE), PIECE), :] = add_hist(q2, c * NX + to, False)

    def piece(i):
        hc[i].wait_recv()
        to = xorder[i]
        return acc[pl.ds(pl.multiple_of(to * PIECE, PIECE), PIECE), :] + hcr[to].astype(F32)

    half = PIECE // 2
    up, down = pl.ds(0, half), pl.ds(half, half)
    hx = [
        copy(HX + 0, hxs.at[0, up], hx1.at[0], xpeer[1]),
        copy(HX + 1, hxs.at[0, down], hx1.at[1], xpeer[3]),
        copy(HX + 2, hxs.at[1, down], hx2.at[0, 1], xpeer[1]),
        copy(HX + 3, hxs.at[2, up], hx2.at[1, 0], xpeer[3]),
        copy(HX + 4, hxsum.at[0], hx2.at[0, 0], xpeer[1]),
        copy(HX + 5, hxsum.at[1], hx2.at[1, 1], xpeer[3]),
    ]
    hxs[0] = piece(0).astype(BF16)
    hx[0].start()
    hx[1].start()
    right = piece(1)
    hxs[1, down, :] = right[half:, :].astype(BF16)
    hx[2].start()
    left = piece(2)
    hxs[2, up, :] = left[:half, :].astype(BF16)
    hx[3].start()
    spare = NX * PIECE
    acc[pl.ds(spare, half), :] = right[:half, :]
    acc[pl.ds(spare + half, half), :] = left[half:, :]
    acc[pl.ds(spare + PIECE, PIECE), :] = piece(3)
    hx[0].wait_recv()
    hxsum[0] = (acc[pl.ds(spare, half), :] + hx1[0].astype(F32)).astype(BF16)
    hx[4].start()
    hx[1].wait_recv()
    hxsum[1] = (acc[pl.ds(spare + half, half), :] + hx1[1].astype(F32)).astype(BF16)
    hx[5].start()

    for cp, d in zip(lzc, (4, 3, 5, 2, 6, 1, 7)):
        arrival(LZ + d - 1, lz.at[step(z, NZ - d, NZ)])
    total = lz[0].astype(F32)
    for i in range(1, NZ):
        total = total + lz[i].astype(F32)
    values = (total[:, :L] / (total[:, L:] + ridge_term)).astype(BF16)
    lv[c, x] = values
    vx = [copy(VX + d - 1, lv.at[c, x], lv.at[c, x], xpeer[d]) for d in (2, 1, 3)]
    for cp in vx:
        cp.start()

    for n in (3, 4, 2, 5):
        hx[n].wait_recv()
    for i, rows in enumerate((up, down)):
        s = acc[pl.ds(spare + PIECE + i * half, half), :] + hx2[0, i].astype(F32) + hx2[1, i].astype(F32)
        acc[pl.ds(i * half, half), :] = s
    hz = []
    for d in (4, 3, 5, 2, 6, 1, 7):
        to = step(z, d, NZ)
        hzs[d - 1] = acc[pl.ds(pl.multiple_of(to * OWN, OWN), OWN), :].astype(BF16)
        hz.append(copy(HZ + d - 1, hzs.at[d - 1], hzr.at[d - 1], zpeer[d]))
        hz[-1].start()

    for d in (2, 1, 3):
        arrival(VX + d - 1, lv.at[c, step(x, NX - d, NX)])
    vc = copy(VC, lv.at[c], lv.at[c], partner)
    vc.start()
    arrival(VC, lv.at[1 - c])

    table = jnp.concatenate([lv[i, j] for i in range(NC) for j in range(NX)], axis=0)
    spot = lax.broadcasted_iota(jnp.int32, (LEAVES, LEAVES), 1)
    label = lax.broadcasted_iota(jnp.int32, (LEAVES, LEAVES), 0)
    swap = jnp.where(owner(spot) == label, 1.0, 0.0).astype(BF16)
    value_ref[...] = jnp.dot(swap, table, preferred_element_type=F32)

    for q in range(NY):
        looked_up = lax.dot_general(hot[q], table, (((0,), (0,)), ((), ())),
                                    preferred_element_type=F32)
        upd_ref[pl.ds(q * Q, Q), :] = (pred[q].astype(F32) + shrinkage * looked_up).astype(BF16)

    s = acc[pl.ds(pl.multiple_of(z * OWN, OWN), OWN), :]
    for i, d in enumerate((4, 3, 5, 2, 6, 1, 7)):
        hz[i].wait_recv()
        s = s + hzr[d - 1].astype(F32)
    hist_ref[...] = s

    for cp in rs + ag + [lc] + lx + lzc + hc + hx + vx + hz + [vc]:
        cp.wait_send()


def local(predictions, labels, feature_codes, leaf_index, sketch_weight):
    vmem = lambda *shape, kind=BF16: pltpu.VMEM(shape, kind)
    hist, values, updated = pl.pallas_call(
        kernel,
        out_shape=(
            jax.ShapeDtypeStruct((OWN, K), F32),
            jax.ShapeDtypeStruct((LEAVES, L), F32),
            jax.ShapeDtypeStruct((R, L), BF16),
        ),
        in_specs=[pl.BlockSpec(memory_space=pl.ANY)] * 5,
        out_specs=[pl.BlockSpec(memory_space=pltpu.VMEM)] * 3,
        scratch_shapes=[
            vmem(NY, Q, L), vmem(NY, Q, L), vmem(F, R, kind=jnp.int32), vmem(1, R, kind=jnp.int32), vmem(L, K),
            vmem(Q, L), vmem(Q, L), vmem(NY, Q, K), vmem(2, H, K), vmem(2, 2, H, K), vmem(2, H, K),
            vmem(NY, Q, K), vmem(NY, LEAVES, Q), vmem(NY, BINS * F, Q),
            vmem(LEAVES, 2 * L, kind=F32), vmem(NX, 8, 2 * L), vmem(NX, 8, 2 * L), vmem(3, 8, 2 * L),
            vmem(3, 8, 2 * L), vmem(NZ, 8, 2 * L), vmem(NC, NX, 8, L),
            vmem(BINS * F, K, kind=F32), vmem(NX, PIECE, K), vmem(NX, PIECE, K), vmem(3, PIECE, K),
            vmem(2, PIECE // 2, K), vmem(2, 2, PIECE // 2, K), vmem(2, PIECE // 2, K),
            vmem(7, OWN, K), vmem(7, OWN, K),
            pltpu.SemaphoreType.DMA((11,)), pltpu.SemaphoreType.DMA((COPIES,)), pltpu.SemaphoreType.DMA((COPIES,)),
        ],
        compiler_params=pltpu.CompilerParams(
            collective_id=0, has_side_effects=True, vmem_limit_bytes=56 * 2**20),
        name="boost",
    )(predictions, labels, feature_codes, leaf_index.reshape(1, R), sketch_weight)
    return hist.reshape(BINS // LEAVES, F, K), values, updated


def solution(mesh):
    return jax.shard_map(
        local,
        mesh=mesh,
        in_specs=(
            P("rows", "feat"),
            P("rows", "feat"),
            P("feat", "rows"),
            P("rows"),
            P("feat", None),
        ),
        out_specs=(P("rows", "feat", None), P(None, "feat"), P("rows", "feat")),
        check_vma=False,
    )
```

```python
import jax
import jax.numpy as jnp
from jax import lax
from jax.experimental import pallas as pl
from jax.experimental.pallas import tpu as pltpu
from jax.sharding import PartitionSpec as P

BINS = 256
LEAVES = 64
NZ, NX, NC, NY = 8, 4, 2, 4
R, L, K, F = 1536, 1024, 256, 8
HALVES = 2
W = K // HALVES
Q = R // NY
H = Q // 2
OWN = BINS // LEAVES * F
PIECE = NZ * OWN
CORE = NX * PIECE
MESH = pl.DeviceIdType.MESH
F32, BF16 = jnp.float32, jnp.bfloat16

shrinkage = 0.5
ridge_term = 1.0

RS, AG, HC, HX, HZ, PER_HALF = 0, 6, 12, 16, 22, 29
LC, LX, LZ, VZ, VX, COPIES = 58, 59, 62, 69, 76, 83
FAR_FIRST = (4, 3, 5, 2, 6, 1, 7)
XORDER = (2, 1, 3, 0)


def leaf_of(slot):
    return (slot & 7) * 8 + ((slot >> 3) & 3) * 2 + (slot >> 5)


def kernel(pred_hbm, lab_hbm, codes_hbm, leaf_hbm, w_hbm,
           hist_ref, value_ref, upd_ref,
           pred, lab, codes, leaf, w, grad, hess, part, rs1, rs2, rsum, sk, hot, oh,
           lsum, lcs, lcr, lxs, lxr, lzs, lzr, lvz, lv,
           acc, hcs, hcr, hxs, hx1, hx2, hxsum, fsum, hzs, hzr,
           load_sem, send, recv):
    row = lax.axis_index("rows")
    y = lax.axis_index("feat")
    c = lax.rem(row, NC)
    x = lax.rem(row // NC, NX)
    z = row // (NC * NX)

    def at(zz, xx, cc):
        return (zz * NX + xx) * NC + cc

    def step(v, d, n):
        return lax.rem(v + d, n)

    partner = (at(z, x, 1 - c), y)
    ypeer = [(row, step(y, d, NY)) for d in range(NY)]
    xpeer = [(at(z, step(x, d, NX), c), y) for d in range(NX)]
    zpeer = [(at(step(z, d, NZ), x, c), y) for d in range(NZ)]
    other = [(at(z, step(x, d, NX), 1 - c), y) for d in range(NX)]
    started = []

    def copy(n, src, dst, to):
        return pltpu.make_async_remote_copy(
            src_ref=src, dst_ref=dst, send_sem=send.at[n], recv_sem=recv.at[n],
            device_id=to, device_id_type=MESH)

    def go(n, src, dst, to):
        cp = copy(n, src, dst, to)
        cp.start()
        started.append(cp)

    def arrival(n, dst):
        copy(n, dst, dst, partner).wait_recv()

    def part_of(start, size, unit):
        return pl.ds(pl.multiple_of(start, unit), size)

    barrier = pltpu.get_barrier_semaphore()
    peers = other + ypeer[1::2] + xpeer[1:] + zpeer[1:]
    for peer in peers:
        pl.semaphore_signal(barrier, inc=1, device_id=peer, device_id_type=MESH)

    order = [step(y, 2, NY), step(y, 1, NY), step(y, 3, NY), y]
    w_load = pltpu.make_async_copy(w_hbm, w, load_sem.at[16])
    leaf_load = pltpu.make_async_copy(leaf_hbm, leaf, load_sem.at[17])
    codes_load = pltpu.make_async_copy(codes_hbm, codes, load_sem.at[18])
    loads = []
    for n in range(2 * NY):
        rows = part_of(order[n // 2] * Q + n % 2 * H, H, H)
        loads.append((
            pltpu.make_async_copy(pred_hbm.at[rows], pred.at[rows], load_sem.at[2 * n]),
            pltpu.make_async_copy(lab_hbm.at[rows], lab.at[rows], load_sem.at[2 * n + 1]),
        ))
        for cp in loads[-1]:
            cp.start()
        if n == 1:
            w_load.start()
    leaf_load.start()
    codes_load.start()

    def block(i):
        q = order[i]
        def rows16(j, carry):
            rows = part_of(q * Q + j * 16, 16, 16)
            logits = pred[rows, :].astype(F32)
            probability = 0.5 + 0.5 * jnp.tanh(0.5 * logits)
            grad[rows, :] = (lab[rows, :].astype(F32) - probability).astype(BF16)
            hess[rows, :] = (probability * (1.0 - probability)).astype(BF16)
            return carry

        for n in range(2):
            for cp in loads[2 * i + n]:
                cp.wait()
            lax.fori_loop(n * H // 16, (n + 1) * H // 16, rows16, 0, unroll=2)
        if i == 0:
            w_load.wait()
        sketch = jnp.dot(grad[part_of(q * Q, Q, Q), :], w[...], preferred_element_type=F32)
        for h in range(HALVES):
            part[h, i] = sketch[:, h * W:(h + 1) * W].astype(BF16)

    top, low = pl.ds(0, H), pl.ds(H, H)

    def rs_first(h):
        go(h * PER_HALF + RS + 0, part.at[h, 0, top], rs1.at[h, 0], ypeer[1])
        go(h * PER_HALF + RS + 1, part.at[h, 0, low], rs1.at[h, 1], ypeer[3])

    def rs_right(h):
        go(h * PER_HALF + RS + 2, part.at[h, 1, low], rs2.at[h, 0, 1], ypeer[1])

    def rs_left(h):
        go(h * PER_HALF + RS + 3, part.at[h, 2, top], rs2.at[h, 1, 0], ypeer[3])

    def rs_sums(h):
        arrival(h * PER_HALF + RS + 0, rs1.at[h, 0])
        rsum[h, 0] = (part[h, 1, top, :].astype(F32) + rs1[h, 0].astype(F32)).astype(BF16)
        go(h * PER_HALF + RS + 4, rsum.at[h, 0], rs2.at[h, 0, 0], ypeer[1])
        arrival(h * PER_HALF + RS + 1, rs1.at[h, 1])
        rsum[h, 1] = (part[h, 2, low, :].astype(F32) + rs1[h, 1].astype(F32)).astype(BF16)
        go(h * PER_HALF + RS + 5, rsum.at[h, 1], rs2.at[h, 1, 1], ypeer[3])

    def sk_at(h, slot, rows):
        return sk.at[h, slot, rows]

    def own_sketch(h):
        for n, rows, s, to, slot in ((0, top, 4, 1, 1), (1, low, 5, 3, 2)):
            arrival(h * PER_HALF + RS + s, rs2.at[h, n, n])
            arrival(h * PER_HALF + RS + (3, 2)[n], rs2.at[h, 1 - n, n])
            total = part[h, 3, rows, :].astype(F32) + rs2[h, 0, n].astype(F32) + rs2[h, 1, n].astype(F32)
            sk[h, 0, rows, :] = total.astype(BF16)
            go(h * PER_HALF + AG + n, sk_at(h, 0, rows), sk_at(h, slot, rows), ypeer[to])

    def own_rest(h):
        go(h * PER_HALF + AG + 2, sk_at(h, 0, low), sk_at(h, 1, low), ypeer[1])
        go(h * PER_HALF + AG + 3, sk_at(h, 0, top), sk_at(h, 2, top), ypeer[3])

    def forward(h):
        arrival(h * PER_HALF + AG + 0, sk_at(h, 1, top))
        go(h * PER_HALF + AG + 4, sk_at(h, 1, top), sk_at(h, 3, top), ypeer[1])
        arrival(h * PER_HALF + AG + 1, sk_at(h, 2, low))
        go(h * PER_HALF + AG + 5, sk_at(h, 2, low), sk_at(h, 3, low), ypeer[3])

    block(0)
    pl.semaphore_wait(barrier, len(peers))
    rs_first(0)
    rs_first(1)
    block(1)
    rs_right(0)
    block(2)
    rs_left(0)
    rs_sums(0)
    rs_right(1)
    rs_left(1)
    block(3)
    rs_sums(1)

    leaf_load.wait()
    lane_owner = leaf_of(lax.broadcasted_iota(jnp.int32, (LEAVES, R), 0))
    here = leaf[...].reshape(1, R) == lane_owner
    hot[...] = jnp.where(here, 1.0, 0.0).astype(BF16)
    for n, src in ((0, grad), (1, hess)):
        lsum[:, n * L:(n + 1) * L] = jnp.dot(hot[...], src[...], preferred_element_type=F32)

    given = lsum[part_of((1 - c) * 32, 32, 32), :].astype(BF16)
    for i in range(NX):
        lcs[i] = given[i * 8:(i + 1) * 8, :]
    go(LC, lcs, lcr, partner)

    own_sketch(0)
    own_rest(0)

    codes_load.wait()
    lanes = [codes[:, part_of(order[i] * Q, Q, 128)] for i in (3, 2, 1, 0)]
    level = jnp.concatenate(lanes, axis=1)
    offset = jnp.where(lax.broadcasted_iota(jnp.int32, (16, R), 0) >= 8, 1, 0)
    pair = (jnp.concatenate([level, level], axis=0) - offset).astype(BF16)

    def bins_of(zz, carry):
        for side in range(NC):
            for i, d in enumerate(XORDER):
                device = at(zz, step(x, d, NX), (1 - c) if side == 0 else c)
                for b in (0, 2):
                    bins = jnp.full((16, 128), device * 4 + b, jnp.int32).astype(BF16)
                    bins = jnp.concatenate([bins] * (R // 128), axis=1)
                    rows = part_of(side * CORE + i * PIECE + zz * OWN + b * 8, 16, 16)
                    oh[rows, :] = jnp.where(pair == bins, jnp.ones((), BF16), jnp.zeros((), BF16))
        return carry

    lax.fori_loop(0, NZ, bins_of, 0)

    arrival(LC, lcr)
    kept = lsum[part_of(c * 32, 32, 32), :]
    for i in range(NX):
        lsum[pl.ds(i * 8, 8), :] = kept[i * 8:(i + 1) * 8, :] + lcr[i].astype(F32)
    for d in (2, 1, 3):
        lxs[d - 1] = lsum[part_of(step(x, d, NX) * 8, 8, 8), :].astype(BF16)
        go(LX + d - 1, lxs.at[d - 1], lxr.at[d - 1], xpeer[d])

    own_sketch(1)
    own_rest(1)

    def terms(h, first, last, rows):
        sketch = sk[h, first:last].reshape((last - first) * Q, W)
        return jnp.dot(oh[rows, first * Q:last * Q], sketch, preferred_element_type=F32)

    tiles = [pl.ds(i * PIECE, PIECE) for i in range(NC * NX)]

    def start_terms(h):
        for rows in tiles:
            acc[h, rows, :] = terms(h, 0, 1, rows)

    def side_terms(h):
        arrival(h * PER_HALF + AG + 2, sk_at(h, 1, low))
        arrival(h * PER_HALF + AG + 3, sk_at(h, 2, top))
        for rows in tiles:
            acc[h, rows, :] = acc[h, rows, :] + terms(h, 1, 3, rows)

    start_terms(0)
    start_terms(1)
    forward(0)
    for d in (1, 2, 3):
        arrival(LX + d - 1, lxr.at[d - 1])
    mine = lsum[part_of(x * 8, 8, 8), :]
    for d in range(3):
        mine = mine + lxr[d].astype(F32)
    for i in range(NZ):
        lzs[i] = mine[i:i + 1, :]
    for d in FAR_FIRST:
        go(LZ + d - 1, lzs.at[step(z, d, NZ)], lzr.at[d - 1], zpeer[d])
    side_terms(0)
    forward(1)
    side_terms(1)

    def last_rows(h):
        arrival(h * PER_HALF + AG + 4, sk_at(h, 3, top))
        arrival(h * PER_HALF + AG + 5, sk_at(h, 3, low))
        for i in range(0, NX, 2):
            for j in (i, i + 1):
                hcs[h, j] = (acc[h, tiles[j], :] + terms(h, 3, 4, tiles[j])).astype(BF16)
            for j in (i, i + 1):
                go(h * PER_HALF + HC + j, hcs.at[h, j], hcr.at[h, j], partner)
        for rows in tiles[NX:]:
            acc[h, rows, :] = acc[h, rows, :] + terms(h, 3, 4, rows)

    half = PIECE // 2
    up, down = pl.ds(0, half), pl.ds(half, half)

    def both_cores(h, i, n):
        return acc[h, pl.ds(CORE + i * PIECE + n * half, half), :] + hcr[h, i, pl.ds(n * half, half), :].astype(F32)

    def x_first(h):
        for i in range(NX):
            arrival(h * PER_HALF + HC + i, hcr.at[h, i])
            if i == 0:
                hxs[h, 0] = both_cores(h, 0, 0).astype(BF16)
                hxs[h, 1] = both_cores(h, 0, 1).astype(BF16)
                go(h * PER_HALF + HX + 0, hxs.at[h, 0], hx1.at[h, 0], xpeer[1])
                go(h * PER_HALF + HX + 1, hxs.at[h, 1], hx1.at[h, 1], xpeer[3])
            if i == 1:
                hxs[h, 2] = both_cores(h, 1, 1).astype(BF16)
                go(h * PER_HALF + HX + 2, hxs.at[h, 2], hx2.at[h, 0, 1], xpeer[1])
            if i == 2:
                hxs[h, 3] = both_cores(h, 2, 0).astype(BF16)
                go(h * PER_HALF + HX + 3, hxs.at[h, 3], hx2.at[h, 1, 0], xpeer[3])

    def x_second(h):
        for n, i, to in ((0, 1, 1), (1, 2, 3)):
            arrival(h * PER_HALF + HX + n, hx1.at[h, n])
            hxsum[h, n] = (both_cores(h, i, n) + hx1[h, n].astype(F32)).astype(BF16)
            go(h * PER_HALF + HX + 4 + n, hxsum.at[h, n], hx2.at[h, n, n], xpeer[to])

    def z_only(h):
        for n in range(2):
            arrival(h * PER_HALF + HX + 4 + n, hx2.at[h, n, n])
            arrival(h * PER_HALF + HX + 3 - n, hx2.at[h, 1 - n, n])
        for n in range(2):
            fsum[h, pl.ds(n * half, half), :] = (
                both_cores(h, 3, n) + hx2[h, 0, n].astype(F32) + hx2[h, 1, n].astype(F32))
        for d in FAR_FIRST:
            hzs[h, d - 1] = fsum[h, part_of(step(z, d, NZ) * OWN, OWN, OWN), :].astype(BF16)
            go(h * PER_HALF + HZ + d - 1, hzs.at[h, d - 1], hzr.at[h, d - 1], zpeer[d])

    def finish(h):
        total = fsum[h, part_of(z * OWN, OWN, OWN), :]
        for d in FAR_FIRST:
            arrival(h * PER_HALF + HZ + d - 1, hzr.at[h, d - 1])
            total = total + hzr[h, d - 1].astype(F32)
        hist_ref[:, h * W:(h + 1) * W] = total

    last_rows(0)
    last_rows(1)

    total = lzs[z]
    for d in FAR_FIRST:
        arrival(LZ + d - 1, lzr.at[d - 1])
        total = total + lzr[d - 1]
    lvz[z] = total[:, :L] / (total[:, L:] + ridge_term)
    for d in FAR_FIRST:
        go(VZ + d - 1, lvz.at[z], lvz.at[z], zpeer[d])

    x_first(0)
    x_first(1)
    x_second(0)
    x_second(1)
    for d in FAR_FIRST:
        arrival(VZ + d - 1, lvz.at[step(z, NZ - d, NZ)])
    lv[c, x] = jnp.concatenate([lvz[i] for i in range(NZ)], axis=0).astype(BF16)
    for d in (2, 1, 3, 0):
        go(VX + 3 + d, lv.at[c, x], lv.at[c, x], other[d])
        if d:
            go(VX + d - 1, lv.at[c, x], lv.at[c, x], xpeer[d])
    z_only(0)
    z_only(1)
    finish(0)
    for d in range(NX):
        arrival(VX + 3 + d, lv.at[1 - c, step(x, NX - d, NX)])
        if d:
            arrival(VX + d - 1, lv.at[c, step(x, NX - d, NX)])

    table = jnp.concatenate([lv[i, j] for i in range(NC) for j in range(NX)], axis=0)
    spot = lax.broadcasted_iota(jnp.int32, (LEAVES, LEAVES), 1)
    label = lax.broadcasted_iota(jnp.int32, (LEAVES, LEAVES), 0)
    swap = jnp.where(leaf_of(spot) == label, 1.0, 0.0).astype(BF16)
    value_ref[...] = jnp.dot(swap, table, preferred_element_type=F32)

    for q in range(NY):
        rows = pl.ds(q * Q, Q)
        looked_up = lax.dot_general(hot[:, rows], table, (((0,), (0,)), ((), ())),
                                    preferred_element_type=F32)
        upd_ref[rows, :] = (pred[rows, :].astype(F32) + shrinkage * looked_up).astype(BF16)
    finish(1)
    for cp in started:
        cp.wait_send()


def store(hist_ref, value_ref, upd_ref, hist_out, value_out, upd_out, sem):
    pairs = ((upd_ref, upd_out), (value_ref, value_out), (hist_ref, hist_out))
    copies = [pltpu.make_async_copy(src, dst, sem.at[i]) for i, (src, dst) in enumerate(pairs)]
    for cp in copies:
        cp.start()
    for cp in copies:
        cp.wait()


def local(predictions, labels, feature_codes, leaf_index, sketch_weight):
    def vmem(*shape, kind=BF16):
        return pltpu.VMEM(shape, kind)

    hist, values, updated = pl.pallas_call(
        kernel,
        out_shape=(vmem(OWN, K, kind=F32), vmem(LEAVES, L, kind=F32), vmem(R, L)),
        in_specs=[pl.BlockSpec(memory_space=pl.ANY)] * 5,
        out_specs=[pl.BlockSpec(memory_space=pltpu.VMEM)] * 3,
        scratch_shapes=[
            vmem(R, L), vmem(R, L), vmem(F, R, kind=jnp.int32), vmem(R, kind=jnp.int32), vmem(L, K),
            vmem(R, L), vmem(R, L), vmem(HALVES, NY, Q, W), vmem(HALVES, 2, H, W), vmem(HALVES, 2, 2, H, W),
            vmem(HALVES, 2, H, W), vmem(HALVES, NY, Q, W), vmem(LEAVES, R), vmem(BINS * F, R),
            vmem(LEAVES, 2 * L, kind=F32), vmem(NX, 8, 2 * L), vmem(NX, 8, 2 * L), vmem(3, 8, 2 * L),
            vmem(3, 8, 2 * L), vmem(NZ, 1, 2 * L, kind=F32), vmem(NZ - 1, 1, 2 * L, kind=F32),
            vmem(NZ, 1, L, kind=F32), vmem(NC, NX, 8, L),
            vmem(HALVES, BINS * F, W, kind=F32), vmem(HALVES, NX, PIECE, W), vmem(HALVES, NX, PIECE, W),
            vmem(HALVES, 4, PIECE // 2, W), vmem(HALVES, 2, PIECE // 2, W), vmem(HALVES, 2, 2, PIECE // 2, W),
            vmem(HALVES, 2, PIECE // 2, W), vmem(HALVES, PIECE, W, kind=F32),
            vmem(HALVES, NZ - 1, OWN, W), vmem(HALVES, NZ - 1, OWN, W),
            pltpu.SemaphoreType.DMA((19,)), pltpu.SemaphoreType.DMA((COPIES,)), pltpu.SemaphoreType.DMA((COPIES,)),
        ],
        compiler_params=pltpu.CompilerParams(
            collective_id=0, has_side_effects=True, vmem_limit_bytes=52 * 2**20),
        name="boost",
    )(predictions, labels, feature_codes, leaf_index, sketch_weight)
    hist, values, updated = pl.pallas_call(
        store,
        out_shape=(
            jax.ShapeDtypeStruct((OWN, K), F32),
            jax.ShapeDtypeStruct((LEAVES, L), F32),
            jax.ShapeDtypeStruct((R, L), BF16),
        ),
        in_specs=[pl.BlockSpec(memory_space=pltpu.VMEM)] * 3,
        out_specs=[pl.BlockSpec(memory_space=pl.ANY)] * 3,
        scratch_shapes=[pltpu.SemaphoreType.DMA((3,))],
        compiler_params=pltpu.CompilerParams(vmem_limit_bytes=2**20),
        name="store",
    )(hist, values, updated)
    return hist.reshape(BINS // LEAVES, F, K), values, updated


def solution(mesh):
    return jax.shard_map(
        local,
        mesh=mesh,
        in_specs=(
            P("rows", "feat"),
            P("rows", "feat"),
            P("feat", "rows"),
            P("rows"),
            P("feat", None),
        ),
        out_specs=(P("rows", "feat", None), P(None, "feat"), P("rows", "feat")),
        check_vma=False,
    )
```

```python
import jax
import jax.numpy as jnp
from jax import lax
from jax.experimental import pallas as pl
from jax.experimental.pallas import tpu as pltpu
from jax.sharding import PartitionSpec as P

BINS = 256
LEAVES = 64
NZ, NX, NC, NY = 8, 4, 2, 4
R, L, K, F = 1536, 1024, 256, 8
HALVES = 2
W = K // HALVES
Q = R // NY
H = Q // 2
OWN = BINS // LEAVES * F
PIECE = NZ * OWN
CORE = NX * PIECE
MESH = pl.DeviceIdType.MESH
F32, BF16 = jnp.float32, jnp.bfloat16

shrinkage = 0.5
ridge_term = 1.0

RS, AG, HC, HX, HZ, PER_HALF = 0, 6, 12, 16, 19, 26
LC, LX, LZ, VZ, VX, COPIES = 52, 53, 56, 63, 70, 77
FAR_FIRST = (4, 3, 5, 2, 6, 1, 7)
XORDER = (2, 1, 3, 0)


def leaf_of(slot):
    return (slot & 7) * 8 + ((slot >> 3) & 3) * 2 + (slot >> 5)


def kernel(pred_hbm, lab_hbm, codes_hbm, leaf_hbm, w_hbm,
           hist_ref, value_ref, upd_ref,
           pred, lab, codes, leaf, w, grad, hess, part, rs1, rs2, rsum, sk, hot, oh,
           lsum, lcs, lcr, lxs, lxr, lzs, lzr, lvz, lv,
           acc, hcs, hcr, hxs, hxr, fsum, hzs, hzr,
           load_sem, send, recv):
    row = lax.axis_index("rows")
    y = lax.axis_index("feat")
    c = lax.rem(row, NC)
    x = lax.rem(row // NC, NX)
    z = row // (NC * NX)

    def at(zz, xx, cc):
        return (zz * NX + xx) * NC + cc

    def step(v, d, n):
        return lax.rem(v + d, n)

    partner = (at(z, x, 1 - c), y)
    ypeer = [(row, step(y, d, NY)) for d in range(NY)]
    xpeer = [(at(z, step(x, d, NX), c), y) for d in range(NX)]
    zpeer = [(at(step(z, d, NZ), x, c), y) for d in range(NZ)]
    other = [(at(z, step(x, d, NX), 1 - c), y) for d in range(NX)]
    started = {}

    def copy(n, src, dst, to):
        return pltpu.make_async_remote_copy(
            src_ref=src, dst_ref=dst, send_sem=send.at[n], recv_sem=recv.at[n],
            device_id=to, device_id_type=MESH)

    def go(n, src, dst, to):
        copy(n, src, dst, to).start()
        started.setdefault(n, (src, dst, to))

    def arrival(n, dst):
        copy(n, dst, dst, partner).wait_recv()

    def part_of(start, size, unit):
        return pl.ds(pl.multiple_of(start, unit), size)

    barrier = pltpu.get_barrier_semaphore()
    peers = other + ypeer[1::2] + xpeer[1:] + zpeer[1:]

    order = [step(y, 2, NY), step(y, 1, NY), step(y, 3, NY), y]
    w_load = pltpu.make_async_copy(w_hbm, w, load_sem.at[16])
    leaf_load = pltpu.make_async_copy(leaf_hbm, leaf, load_sem.at[17])
    codes_load = pltpu.make_async_copy(codes_hbm, codes, load_sem.at[18])
    loads = []
    for n in range(2 * NY):
        rows = part_of(order[n // 2] * Q + n % 2 * H, H, H)
        loads.append((
            pltpu.make_async_copy(pred_hbm.at[rows], pred.at[rows], load_sem.at[2 * n]),
            pltpu.make_async_copy(lab_hbm.at[rows], lab.at[rows], load_sem.at[2 * n + 1]),
        ))
        for cp in loads[-1]:
            cp.start()
        if n == 1:
            w_load.start()
            for peer in peers:
                pl.semaphore_signal(barrier, inc=1, device_id=peer, device_id_type=MESH)
    leaf_load.start()
    codes_load.start()

    def block(i):
        q = order[i]
        def rows16(j, carry):
            rows = part_of(q * Q + j * 16, 16, 16)
            logits = pred[rows, :].astype(F32)
            probability = 0.5 + 0.5 * jnp.tanh(0.5 * logits)
            grad[rows, :] = (lab[rows, :].astype(F32) - probability).astype(BF16)
            hess[rows, :] = (probability * (1.0 - probability)).astype(BF16)
            return carry

        for n in range(2):
            for cp in loads[2 * i + n]:
                cp.wait()
            lax.fori_loop(n * H // 16, (n + 1) * H // 16, rows16, 0, unroll=2)
        if i == 0:
            w_load.wait()
        sketch = jnp.dot(grad[part_of(q * Q, Q, Q), :], w[...], preferred_element_type=F32)
        for h in range(HALVES):
            part[h, i] = sketch[:, h * W:(h + 1) * W].astype(BF16)

    top, low = pl.ds(0, H), pl.ds(H, H)

    def rs_first(h):
        go(h * PER_HALF + RS + 0, part.at[h, 0, top], rs1.at[h, 0], ypeer[1])
        go(h * PER_HALF + RS + 1, part.at[h, 0, low], rs1.at[h, 1], ypeer[3])

    def rs_right(h):
        go(h * PER_HALF + RS + 2, part.at[h, 1, low], rs2.at[h, 0, 1], ypeer[1])

    def rs_left(h):
        go(h * PER_HALF + RS + 3, part.at[h, 2, top], rs2.at[h, 1, 0], ypeer[3])

    def rs_sums(h):
        arrival(h * PER_HALF + RS + 0, rs1.at[h, 0])
        rsum[h, 0] = (part[h, 1, top, :].astype(F32) + rs1[h, 0].astype(F32)).astype(BF16)
        go(h * PER_HALF + RS + 4, rsum.at[h, 0], rs2.at[h, 0, 0], ypeer[1])
        arrival(h * PER_HALF + RS + 1, rs1.at[h, 1])
        rsum[h, 1] = (part[h, 2, low, :].astype(F32) + rs1[h, 1].astype(F32)).astype(BF16)
        go(h * PER_HALF + RS + 5, rsum.at[h, 1], rs2.at[h, 1, 1], ypeer[3])

    def sk_at(h, slot, rows):
        return sk.at[h, slot, rows]

    def own_sketch(h):
        for n, rows, s, to, slot in ((0, top, 4, 1, 1), (1, low, 5, 3, 2)):
            arrival(h * PER_HALF + RS + s, rs2.at[h, n, n])
            arrival(h * PER_HALF + RS + (3, 2)[n], rs2.at[h, 1 - n, n])
            total = part[h, 3, rows, :].astype(F32) + rs2[h, 0, n].astype(F32) + rs2[h, 1, n].astype(F32)
            sk[h, 0, rows, :] = total.astype(BF16)
            go(h * PER_HALF + AG + n, sk_at(h, 0, rows), sk_at(h, slot, rows), ypeer[to])

    def own_rest(h):
        go(h * PER_HALF + AG + 2, sk_at(h, 0, low), sk_at(h, 1, low), ypeer[1])
        go(h * PER_HALF + AG + 3, sk_at(h, 0, top), sk_at(h, 2, top), ypeer[3])

    def forward(h):
        arrival(h * PER_HALF + AG + 0, sk_at(h, 1, top))
        go(h * PER_HALF + AG + 4, sk_at(h, 1, top), sk_at(h, 3, top), ypeer[1])
        arrival(h * PER_HALF + AG + 1, sk_at(h, 2, low))
        go(h * PER_HALF + AG + 5, sk_at(h, 2, low), sk_at(h, 3, low), ypeer[3])

    block(0)
    pl.semaphore_wait(barrier, len(peers))
    rs_first(0)
    rs_first(1)
    block(1)
    rs_right(0)
    block(2)
    rs_left(0)
    rs_sums(0)
    rs_right(1)
    rs_left(1)
    block(3)
    rs_sums(1)

    leaf_load.wait()
    lane_owner = leaf_of(lax.broadcasted_iota(jnp.int32, (LEAVES, R), 0))
    here = leaf[...].reshape(1, R) == lane_owner
    hot[...] = jnp.where(here, 1.0, 0.0).astype(BF16)
    for n, src in ((0, grad), (1, hess)):
        lsum[:, n * L:(n + 1) * L] = jnp.dot(hot[...], src[...], preferred_element_type=F32)

    given = lsum[part_of((1 - c) * 32, 32, 32), :].astype(BF16)
    for i in range(NX):
        lcs[i] = given[i * 8:(i + 1) * 8, :]
    go(LC, lcs, lcr, partner)

    own_sketch(0)
    own_rest(0)

    codes_load.wait()
    lanes = [codes[:, part_of(order[i] * Q, Q, 128)] for i in (3, 2, 1, 0)]
    level = jnp.concatenate(lanes, axis=1)
    offset = jnp.where(lax.broadcasted_iota(jnp.int32, (16, R), 0) >= 8, 1, 0)
    pair = (jnp.concatenate([level, level], axis=0) - offset).astype(BF16)

    def bins_of(zz, carry):
        for side in range(NC):
            for i, d in enumerate(XORDER):
                device = at(zz, step(x, d, NX), (1 - c) if side == 0 else c)
                for b in (0, 2):
                    bins = jnp.full((16, 128), device * 4 + b, jnp.int32).astype(BF16)
                    bins = jnp.concatenate([bins] * (R // 128), axis=1)
                    rows = part_of(side * CORE + i * PIECE + zz * OWN + b * 8, 16, 16)
                    oh[rows, :] = jnp.where(pair == bins, jnp.ones((), BF16), jnp.zeros((), BF16))
        return carry

    lax.fori_loop(0, NZ, bins_of, 0)

    arrival(LC, lcr)
    kept = lsum[part_of(c * 32, 32, 32), :]
    for i in range(NX):
        lsum[pl.ds(i * 8, 8), :] = kept[i * 8:(i + 1) * 8, :] + lcr[i].astype(F32)
    for d in (2, 1, 3):
        lxs[d - 1] = lsum[part_of(step(x, d, NX) * 8, 8, 8), :].astype(BF16)
        go(LX + d - 1, lxs.at[d - 1], lxr.at[d - 1], xpeer[d])

    own_sketch(1)
    own_rest(1)

    def terms(h, first, last, rows):
        sketch = sk[h, first:last].reshape((last - first) * Q, W)
        return jnp.dot(oh[rows, first * Q:last * Q], sketch, preferred_element_type=F32)

    tiles = [pl.ds(i * PIECE, PIECE) for i in range(NC * NX)]

    def start_terms(h):
        for rows in tiles:
            acc[h, rows, :] = terms(h, 0, 1, rows)

    def side_terms(h):
        arrival(h * PER_HALF + AG + 2, sk_at(h, 1, low))
        arrival(h * PER_HALF + AG + 3, sk_at(h, 2, top))
        for rows in tiles:
            acc[h, rows, :] = acc[h, rows, :] + terms(h, 1, 3, rows)

    start_terms(0)
    forward(0)
    start_terms(1)
    side_terms(0)
    forward(1)
    for d in (1, 2, 3):
        arrival(LX + d - 1, lxr.at[d - 1])
    mine = lsum[part_of(x * 8, 8, 8), :]
    for d in range(3):
        mine = mine + lxr[d].astype(F32)
    for i in range(NZ):
        lzs[i] = mine[i:i + 1, :]
    for d in FAR_FIRST:
        go(LZ + d - 1, lzs.at[step(z, d, NZ)], lzr.at[d - 1], zpeer[d])

    def last_rows(h):
        arrival(h * PER_HALF + AG + 4, sk_at(h, 3, top))
        arrival(h * PER_HALF + AG + 5, sk_at(h, 3, low))
        for i in range(0, NX, 2):
            for j in (i, i + 1):
                hcs[h, j] = (acc[h, tiles[j], :] + terms(h, 3, 4, tiles[j])).astype(BF16)
            for j in (i, i + 1):
                go(h * PER_HALF + HC + j, hcs.at[h, j], hcr.at[h, j], partner)
        for rows in tiles[NX:]:
            acc[h, rows, :] = acc[h, rows, :] + terms(h, 3, 4, rows)

    def both_cores(h, i):
        return acc[h, tiles[NX + i], :] + hcr[h, i].astype(F32)

    def x_only(h):
        for i, d in enumerate(XORDER):
            arrival(h * PER_HALF + HC + i, hcr.at[h, i])
            if d:
                hxs[h, i] = both_cores(h, i).astype(BF16)
                go(h * PER_HALF + HX + i, hxs.at[h, i], hxr.at[h, i], xpeer[d])

    def z_only(h):
        total = both_cores(h, NX - 1)
        for i in range(NX - 1):
            arrival(h * PER_HALF + HX + i, hxr.at[h, i])
            total = total + hxr[h, i].astype(F32)
        fsum[h] = total
        for d in FAR_FIRST:
            hzs[h, d - 1] = fsum[h, part_of(step(z, d, NZ) * OWN, OWN, OWN), :].astype(BF16)
            go(h * PER_HALF + HZ + d - 1, hzs.at[h, d - 1], hzr.at[h, d - 1], zpeer[d])

    def finish(h):
        total = fsum[h, part_of(z * OWN, OWN, OWN), :]
        for d in FAR_FIRST:
            arrival(h * PER_HALF + HZ + d - 1, hzr.at[h, d - 1])
            total = total + hzr[h, d - 1].astype(F32)
        hist_ref[:, h * W:(h + 1) * W] = total

    for i, d in enumerate(XORDER[:NX - 1]):
        started[HX + i] = (hxs.at[0, i], hxr.at[0, i], xpeer[d])
    last_rows(0)
    side_terms(1)
    pl.when(c == 0)(lambda: x_only(0))
    last_rows(1)
    pl.when(c == 1)(lambda: x_only(0))

    total = lzs[z]
    for d in FAR_FIRST:
        arrival(LZ + d - 1, lzr.at[d - 1])
        total = total + lzr[d - 1]
    lvz[z] = total[:, :L] / (total[:, L:] + ridge_term)
    for d in FAR_FIRST:
        go(VZ + d - 1, lvz.at[z], lvz.at[z], zpeer[d])

    x_only(1)

    for d in FAR_FIRST:
        arrival(VZ + d - 1, lvz.at[step(z, NZ - d, NZ)])
    lv[c, x] = jnp.concatenate([lvz[i] for i in range(NZ)], axis=0).astype(BF16)
    for d in (2, 1, 3, 0):
        go(VX + 3 + d, lv.at[c, x], lv.at[c, x], other[d])
        if d:
            go(VX + d - 1, lv.at[c, x], lv.at[c, x], xpeer[d])
    z_only(0)
    z_only(1)
    for d in range(NX):
        arrival(VX + 3 + d, lv.at[1 - c, step(x, NX - d, NX)])
        if d:
            arrival(VX + d - 1, lv.at[c, step(x, NX - d, NX)])

    table = jnp.concatenate([lv[i, j] for i in range(NC) for j in range(NX)], axis=0)
    spot = lax.broadcasted_iota(jnp.int32, (LEAVES, LEAVES), 1)
    label = lax.broadcasted_iota(jnp.int32, (LEAVES, LEAVES), 0)
    swap = jnp.where(leaf_of(spot) == label, 1.0, 0.0).astype(BF16)
    value_ref[...] = jnp.dot(swap, table, preferred_element_type=F32)

    for q in range(NY):
        rows = pl.ds(q * Q, Q)
        looked_up = lax.dot_general(hot[:, rows], table, (((0,), (0,)), ((), ())),
                                    preferred_element_type=F32)
        upd_ref[rows, :] = (pred[rows, :].astype(F32) + shrinkage * looked_up).astype(BF16)
    finish(0)
    finish(1)
    for n, (src, dst, to) in started.items():
        copy(n, src, dst, to).wait_send()


def store(hist_ref, value_ref, upd_ref, hist_out, value_out, upd_out, sem):
    blocks = [pl.ds(i * Q, Q) for i in range(NY)]
    pairs = [(upd_ref.at[rows], upd_out.at[rows]) for rows in blocks]
    pairs += [(value_ref, value_out), (hist_ref, hist_out)]
    copies = [pltpu.make_async_copy(src, dst, sem.at[i]) for i, (src, dst) in enumerate(pairs)]
    for cp in copies:
        cp.start()
    for cp in copies:
        cp.wait()


def local(predictions, labels, feature_codes, leaf_index, sketch_weight):
    def vmem(*shape, kind=BF16):
        return pltpu.VMEM(shape, kind)

    hist, values, updated = pl.pallas_call(
        kernel,
        out_shape=(vmem(OWN, K, kind=F32), vmem(LEAVES, L, kind=F32), vmem(R, L)),
        in_specs=[pl.BlockSpec(memory_space=pl.ANY)] * 5,
        out_specs=[pl.BlockSpec(memory_space=pltpu.VMEM)] * 3,
        scratch_shapes=[
            vmem(R, L), vmem(R, L), vmem(F, R, kind=jnp.int32), vmem(R, kind=jnp.int32), vmem(L, K),
            vmem(R, L), vmem(R, L), vmem(HALVES, NY, Q, W), vmem(HALVES, 2, H, W), vmem(HALVES, 2, 2, H, W),
            vmem(HALVES, 2, H, W), vmem(HALVES, NY, Q, W), vmem(LEAVES, R), vmem(BINS * F, R),
            vmem(LEAVES, 2 * L, kind=F32), vmem(NX, 8, 2 * L), vmem(NX, 8, 2 * L), vmem(3, 8, 2 * L),
            vmem(3, 8, 2 * L), vmem(NZ, 1, 2 * L, kind=F32), vmem(NZ - 1, 1, 2 * L, kind=F32),
            vmem(NZ, 1, L, kind=F32), vmem(NC, NX, 8, L),
            vmem(HALVES, BINS * F, W, kind=F32), vmem(HALVES, NX, PIECE, W), vmem(HALVES, NX, PIECE, W),
            vmem(HALVES, NX - 1, PIECE, W), vmem(HALVES, NX - 1, PIECE, W), vmem(HALVES, PIECE, W, kind=F32),
            vmem(HALVES, NZ - 1, OWN, W), vmem(HALVES, NZ - 1, OWN, W),
            pltpu.SemaphoreType.DMA((19,)), pltpu.SemaphoreType.DMA((COPIES,)), pltpu.SemaphoreType.DMA((COPIES,)),
        ],
        compiler_params=pltpu.CompilerParams(
            collective_id=0, has_side_effects=True, vmem_limit_bytes=52 * 2**20),
        name="boost",
    )(predictions, labels, feature_codes, leaf_index, sketch_weight)
    hist, values, updated = pl.pallas_call(
        store,
        out_shape=(
            jax.ShapeDtypeStruct((OWN, K), F32),
            jax.ShapeDtypeStruct((LEAVES, L), F32),
            jax.ShapeDtypeStruct((R, L), BF16),
        ),
        in_specs=[pl.BlockSpec(memory_space=pltpu.VMEM)] * 3,
        out_specs=[pl.BlockSpec(memory_space=pl.ANY)] * 3,
        scratch_shapes=[pltpu.SemaphoreType.DMA((NY + 2,))],
        compiler_params=pltpu.CompilerParams(vmem_limit_bytes=2**20),
        name="store",
    )(hist, values, updated)
    return hist.reshape(BINS // LEAVES, F, K), values, updated


def solution(mesh):
    return jax.shard_map(
        local,
        mesh=mesh,
        in_specs=(
            P("rows", "feat"),
            P("rows", "feat"),
            P("feat", "rows"),
            P("rows"),
            P("feat", None),
        ),
        out_specs=(P("rows", "feat", None), P(None, "feat"), P("rows", "feat")),
        check_vma=False,
    )
```

```python
import jax
import jax.numpy as jnp
from jax import lax
from jax.experimental import pallas as pl
from jax.experimental.pallas import tpu as pltpu
from jax.sharding import PartitionSpec as P

BINS = 256
LEAVES = 64
NZ, NX, NC, NY = 8, 4, 2, 4
R, L, K, F = 1536, 1024, 256, 8
HALVES = 2
W = K // HALVES
Q = R // NY
H = Q // 2
OWN = BINS // LEAVES * F
PIECE = NZ * OWN
CORE = NX * PIECE
MESH = pl.DeviceIdType.MESH
F32, BF16 = jnp.float32, jnp.bfloat16

shrinkage = 0.5
ridge_term = 1.0

RS, AG, HC, HX, HZ, PER_HALF = 0, 6, 12, 16, 19, 26
LC, LX, LZ, VZ, VX, COPIES = 52, 53, 56, 63, 70, 77
FAR_FIRST = (4, 3, 5, 2, 6, 1, 7)
XORDER = (2, 1, 3, 0)


def leaf_of(slot):
    return (slot & 7) * 8 + ((slot >> 3) & 3) * 2 + (slot >> 5)


def kernel(pred_hbm, lab_hbm, codes_hbm, leaf_hbm, w_hbm,
           hist_ref, value_ref, upd_ref,
           pred, lab, codes, leaf, w, grad, hess, part, rs1, rs2, rsum, sk, hot, oh,
           lsum, lcs, lcr, lxs, lxr, lzs, lzr, lvz, lv,
           acc, hcs, hcr, hxs, hxr, fsum, hzs, hzr,
           load_sem, send, recv):
    row = lax.axis_index("rows")
    y = lax.axis_index("feat")
    c = lax.rem(row, NC)
    x = lax.rem(row // NC, NX)
    z = row // (NC * NX)

    def at(zz, xx, cc):
        return (zz * NX + xx) * NC + cc

    def step(v, d, n):
        return lax.rem(v + d, n)

    partner = (at(z, x, 1 - c), y)
    ypeer = [(row, step(y, d, NY)) for d in range(NY)]
    xpeer = [(at(z, step(x, d, NX), c), y) for d in range(NX)]
    zpeer = [(at(step(z, d, NZ), x, c), y) for d in range(NZ)]
    other = [(at(z, step(x, d, NX), 1 - c), y) for d in range(NX)]
    started = {}

    def copy(n, src, dst, to):
        return pltpu.make_async_remote_copy(
            src_ref=src, dst_ref=dst, send_sem=send.at[n], recv_sem=recv.at[n],
            device_id=to, device_id_type=MESH)

    def go(n, src, dst, to):
        copy(n, src, dst, to).start()
        started.setdefault(n, (src, dst, to))

    def arrival(n, dst):
        copy(n, dst, dst, partner).wait_recv()

    def part_of(start, size, unit):
        return pl.ds(pl.multiple_of(start, unit), size)

    barrier = pltpu.get_barrier_semaphore()
    peers = other + ypeer[1::2] + xpeer[1:] + zpeer[1:]

    order = [step(y, 2, NY), step(y, 1, NY), step(y, 3, NY), y]
    w_load = pltpu.make_async_copy(w_hbm, w, load_sem.at[16])
    leaf_load = pltpu.make_async_copy(leaf_hbm, leaf, load_sem.at[17])
    codes_load = pltpu.make_async_copy(codes_hbm, codes, load_sem.at[18])
    loads = []
    for n in range(2 * NY):
        rows = part_of(order[n // 2] * Q + n % 2 * H, H, H)
        loads.append((
            pltpu.make_async_copy(pred_hbm.at[rows], pred.at[rows], load_sem.at[2 * n]),
            pltpu.make_async_copy(lab_hbm.at[rows], lab.at[rows], load_sem.at[2 * n + 1]),
        ))
        for cp in loads[-1]:
            cp.start()
        if n == 1:
            w_load.start()
            for peer in peers:
                pl.semaphore_signal(barrier, inc=1, device_id=peer, device_id_type=MESH)
    leaf_load.start()
    codes_load.start()

    def block(i):
        q = order[i]
        def rows16(j, carry):
            rows = part_of(q * Q + j * 16, 16, 16)
            logits = pred[rows, :].astype(F32)
            probability = 0.5 + 0.5 * jnp.tanh(0.5 * logits)
            grad[rows, :] = (lab[rows, :].astype(F32) - probability).astype(BF16)
            hess[rows, :] = (probability * (1.0 - probability)).astype(BF16)
            return carry

        for n in range(2):
            for cp in loads[2 * i + n]:
                cp.wait()
            lax.fori_loop(n * H // 16, (n + 1) * H // 16, rows16, 0, unroll=2)
        if i == 0:
            w_load.wait()
        sketch = jnp.dot(grad[part_of(q * Q, Q, Q), :], w[...], preferred_element_type=F32)
        for h in range(HALVES):
            part[h, i] = sketch[:, h * W:(h + 1) * W].astype(BF16)

    top, low = pl.ds(0, H), pl.ds(H, H)

    def rs_first(h):
        go(h * PER_HALF + RS + 0, part.at[h, 0, top], rs1.at[h, 0], ypeer[1])
        go(h * PER_HALF + RS + 1, part.at[h, 0, low], rs1.at[h, 1], ypeer[3])

    def rs_right(h):
        go(h * PER_HALF + RS + 2, part.at[h, 1, low], rs2.at[h, 0, 1], ypeer[1])

    def rs_left(h):
        go(h * PER_HALF + RS + 3, part.at[h, 2, top], rs2.at[h, 1, 0], ypeer[3])

    def rs_sums(h):
        arrival(h * PER_HALF + RS + 0, rs1.at[h, 0])
        rsum[h, 0] = (part[h, 1, top, :].astype(F32) + rs1[h, 0].astype(F32)).astype(BF16)
        go(h * PER_HALF + RS + 4, rsum.at[h, 0], rs2.at[h, 0, 0], ypeer[1])
        arrival(h * PER_HALF + RS + 1, rs1.at[h, 1])
        rsum[h, 1] = (part[h, 2, low, :].astype(F32) + rs1[h, 1].astype(F32)).astype(BF16)
        go(h * PER_HALF + RS + 5, rsum.at[h, 1], rs2.at[h, 1, 1], ypeer[3])

    def sk_at(h, slot, rows):
        return sk.at[h, slot, rows]

    def own_sketch(h):
        for n, rows, s, to, slot in ((0, top, 4, 1, 1), (1, low, 5, 3, 2)):
            arrival(h * PER_HALF + RS + s, rs2.at[h, n, n])
            arrival(h * PER_HALF + RS + (3, 2)[n], rs2.at[h, 1 - n, n])
            total = part[h, 3, rows, :].astype(F32) + rs2[h, 0, n].astype(F32) + rs2[h, 1, n].astype(F32)
            sk[h, 0, rows, :] = total.astype(BF16)
            go(h * PER_HALF + AG + n, sk_at(h, 0, rows), sk_at(h, slot, rows), ypeer[to])

    def own_rest(h):
        go(h * PER_HALF + AG + 2, sk_at(h, 0, low), sk_at(h, 1, low), ypeer[1])
        go(h * PER_HALF + AG + 3, sk_at(h, 0, top), sk_at(h, 2, top), ypeer[3])

    def forward(h):
        arrival(h * PER_HALF + AG + 0, sk_at(h, 1, top))
        go(h * PER_HALF + AG + 4, sk_at(h, 1, top), sk_at(h, 3, top), ypeer[1])
        arrival(h * PER_HALF + AG + 1, sk_at(h, 2, low))
        go(h * PER_HALF + AG + 5, sk_at(h, 2, low), sk_at(h, 3, low), ypeer[3])

    block(0)
    pl.semaphore_wait(barrier, len(peers))
    rs_first(0)
    rs_first(1)
    block(1)
    rs_right(0)
    block(2)
    rs_left(0)
    rs_sums(0)
    rs_right(1)
    rs_left(1)
    block(3)
    rs_sums(1)

    leaf_load.wait()
    lane_owner = leaf_of(lax.broadcasted_iota(jnp.int32, (LEAVES, R), 0))
    here = leaf[...].reshape(1, R) == lane_owner
    hot[...] = jnp.where(here, 1.0, 0.0).astype(BF16)
    for n, src in ((0, grad), (1, hess)):
        lsum[:, n * L:(n + 1) * L] = jnp.dot(hot[...], src[...], preferred_element_type=F32)

    given = lsum[part_of((1 - c) * 32, 32, 32), :].astype(BF16)
    for i in range(NX):
        lcs[i] = given[i * 8:(i + 1) * 8, :]
    go(LC, lcs, lcr, partner)

    own_sketch(0)
    own_rest(0)

    codes_load.wait()
    lanes = [codes[:, part_of(order[i] * Q, Q, 128)] for i in (3, 2, 1, 0)]
    level = jnp.concatenate(lanes, axis=1)
    offset = jnp.where(lax.broadcasted_iota(jnp.int32, (16, R), 0) >= 8, 1, 0)
    pair = (jnp.concatenate([level, level], axis=0) - offset).astype(BF16)

    def bins_of(zz, carry):
        for side in range(NC):
            for i, d in enumerate(XORDER):
                device = at(zz, step(x, d, NX), (1 - c) if side == 0 else c)
                for b in (0, 2):
                    bins = jnp.full((16, 128), device * 4 + b, jnp.int32).astype(BF16)
                    bins = jnp.concatenate([bins] * (R // 128), axis=1)
                    rows = part_of(side * CORE + i * PIECE + zz * OWN + b * 8, 16, 16)
                    oh[rows, :] = jnp.where(pair == bins, jnp.ones((), BF16), jnp.zeros((), BF16))
        return carry

    lax.fori_loop(0, NZ, bins_of, 0)

    for d in (1, 2, 3):
        started[LX + d - 1] = (lxs.at[d - 1], lxr.at[d - 1], xpeer[d])

    def leaf_x():
        arrival(LC, lcr)
        kept = lsum[part_of(c * 32, 32, 32), :]
        for i in range(NX):
            lsum[pl.ds(i * 8, 8), :] = kept[i * 8:(i + 1) * 8, :] + lcr[i].astype(F32)
        for d in (2, 1, 3):
            lxs[d - 1] = lsum[part_of(step(x, d, NX) * 8, 8, 8), :].astype(BF16)
            go(LX + d - 1, lxs.at[d - 1], lxr.at[d - 1], xpeer[d])

    pl.when(c == 0)(leaf_x)
    own_sketch(1)
    own_rest(1)
    pl.when(c == 1)(leaf_x)

    def terms(h, first, last, rows):
        sketch = sk[h, first:last].reshape((last - first) * Q, W)
        return jnp.dot(oh[rows, first * Q:last * Q], sketch, preferred_element_type=F32)

    tiles = [pl.ds(i * PIECE, PIECE) for i in range(NC * NX)]

    def start_terms(h):
        for rows in tiles:
            acc[h, rows, :] = terms(h, 0, 1, rows)

    def side_terms(h):
        arrival(h * PER_HALF + AG + 2, sk_at(h, 1, low))
        arrival(h * PER_HALF + AG + 3, sk_at(h, 2, top))
        for rows in tiles:
            acc[h, rows, :] = acc[h, rows, :] + terms(h, 1, 3, rows)

    start_terms(0)
    forward(0)
    start_terms(1)
    side_terms(0)
    forward(1)
    for d in (1, 2, 3):
        arrival(LX + d - 1, lxr.at[d - 1])
    mine = lsum[part_of(x * 8, 8, 8), :]
    for d in range(3):
        mine = mine + lxr[d].astype(F32)
    for i in range(NZ):
        lzs[i] = mine[i:i + 1, :]
    for d in FAR_FIRST:
        go(LZ + d - 1, lzs.at[step(z, d, NZ)], lzr.at[d - 1], zpeer[d])

    def last_rows(h):
        arrival(h * PER_HALF + AG + 4, sk_at(h, 3, top))
        arrival(h * PER_HALF + AG + 5, sk_at(h, 3, low))
        for i in range(0, NX, 2):
            for j in (i, i + 1):
                hcs[h, j] = (acc[h, tiles[j], :] + terms(h, 3, 4, tiles[j])).astype(BF16)
            for j in (i, i + 1):
                go(h * PER_HALF + HC + j, hcs.at[h, j], hcr.at[h, j], partner)
        for rows in tiles[NX:]:
            acc[h, rows, :] = acc[h, rows, :] + terms(h, 3, 4, rows)

    def both_cores(h, i):
        return acc[h, tiles[NX + i], :] + hcr[h, i].astype(F32)

    def x_only(h):
        for i, d in enumerate(XORDER):
            arrival(h * PER_HALF + HC + i, hcr.at[h, i])
            if d:
                hxs[h, i] = both_cores(h, i).astype(BF16)
                go(h * PER_HALF + HX + i, hxs.at[h, i], hxr.at[h, i], xpeer[d])

    def z_only(h):
        total = both_cores(h, NX - 1)
        for i in range(NX - 1):
            arrival(h * PER_HALF + HX + i, hxr.at[h, i])
            total = total + hxr[h, i].astype(F32)
        fsum[h] = total
        for d in FAR_FIRST:
            hzs[h, d - 1] = fsum[h, part_of(step(z, d, NZ) * OWN, OWN, OWN), :].astype(BF16)
            go(h * PER_HALF + HZ + d - 1, hzs.at[h, d - 1], hzr.at[h, d - 1], zpeer[d])

    def finish(h):
        total = fsum[h, part_of(z * OWN, OWN, OWN), :]
        for d in FAR_FIRST:
            arrival(h * PER_HALF + HZ + d - 1, hzr.at[h, d - 1])
            total = total + hzr[h, d - 1].astype(F32)
        hist_ref[:, h * W:(h + 1) * W] = total

    for i, d in enumerate(XORDER[:NX - 1]):
        started[HX + i] = (hxs.at[0, i], hxr.at[0, i], xpeer[d])
    last_rows(0)
    side_terms(1)
    pl.when(c == 0)(lambda: x_only(0))
    last_rows(1)
    pl.when(c == 1)(lambda: x_only(0))

    total = lzs[z]
    for d in FAR_FIRST:
        arrival(LZ + d - 1, lzr.at[d - 1])
        total = total + lzr[d - 1]
    lvz[z] = total[:, :L] / (total[:, L:] + ridge_term)
    for d in FAR_FIRST:
        go(VZ + d - 1, lvz.at[z], lvz.at[z], zpeer[d])

    x_only(1)

    for d in FAR_FIRST:
        arrival(VZ + d - 1, lvz.at[step(z, NZ - d, NZ)])
    lv[c, x] = jnp.concatenate([lvz[i] for i in range(NZ)], axis=0).astype(BF16)
    for d in (2, 1, 3, 0):
        go(VX + 3 + d, lv.at[c, x], lv.at[c, x], other[d])
        if d:
            go(VX + d - 1, lv.at[c, x], lv.at[c, x], xpeer[d])
    z_only(0)
    z_only(1)
    for d in range(NX):
        arrival(VX + 3 + d, lv.at[1 - c, step(x, NX - d, NX)])
        if d:
            arrival(VX + d - 1, lv.at[c, step(x, NX - d, NX)])

    table = jnp.concatenate([lv[i, j] for i in range(NC) for j in range(NX)], axis=0)
    spot = lax.broadcasted_iota(jnp.int32, (LEAVES, LEAVES), 1)
    label = lax.broadcasted_iota(jnp.int32, (LEAVES, LEAVES), 0)
    swap = jnp.where(leaf_of(spot) == label, 1.0, 0.0).astype(BF16)
    value_ref[...] = jnp.dot(swap, table, preferred_element_type=F32)

    for q in range(NY):
        rows = pl.ds(q * Q, Q)
        looked_up = lax.dot_general(hot[:, rows], table, (((0,), (0,)), ((), ())),
                                    preferred_element_type=F32)
        upd_ref[rows, :] = (pred[rows, :].astype(F32) + shrinkage * looked_up).astype(BF16)
    finish(0)
    finish(1)
    for n, (src, dst, to) in started.items():
        copy(n, src, dst, to).wait_send()


def store(hist_ref, value_ref, upd_ref, hist_out, value_out, upd_out, sem):
    blocks = [pl.ds(i * Q, Q) for i in range(NY)]
    pairs = [(upd_ref.at[rows], upd_out.at[rows]) for rows in blocks]
    pairs += [(value_ref, value_out), (hist_ref, hist_out)]
    copies = [pltpu.make_async_copy(src, dst, sem.at[i]) for i, (src, dst) in enumerate(pairs)]
    for cp in copies:
        cp.start()
    for cp in copies:
        cp.wait()


def local(predictions, labels, feature_codes, leaf_index, sketch_weight):
    def vmem(*shape, kind=BF16):
        return pltpu.VMEM(shape, kind)

    hist, values, updated = pl.pallas_call(
        kernel,
        out_shape=(vmem(OWN, K, kind=F32), vmem(LEAVES, L, kind=F32), vmem(R, L)),
        in_specs=[pl.BlockSpec(memory_space=pl.ANY)] * 5,
        out_specs=[pl.BlockSpec(memory_space=pltpu.VMEM)] * 3,
        scratch_shapes=[
            vmem(R, L), vmem(R, L), vmem(F, R, kind=jnp.int32), vmem(R, kind=jnp.int32), vmem(L, K),
            vmem(R, L), vmem(R, L), vmem(HALVES, NY, Q, W), vmem(HALVES, 2, H, W), vmem(HALVES, 2, 2, H, W),
            vmem(HALVES, 2, H, W), vmem(HALVES, NY, Q, W), vmem(LEAVES, R), vmem(BINS * F, R),
            vmem(LEAVES, 2 * L, kind=F32), vmem(NX, 8, 2 * L), vmem(NX, 8, 2 * L), vmem(3, 8, 2 * L),
            vmem(3, 8, 2 * L), vmem(NZ, 1, 2 * L, kind=F32), vmem(NZ - 1, 1, 2 * L, kind=F32),
            vmem(NZ, 1, L, kind=F32), vmem(NC, NX, 8, L),
            vmem(HALVES, BINS * F, W, kind=F32), vmem(HALVES, NX, PIECE, W), vmem(HALVES, NX, PIECE, W),
            vmem(HALVES, NX - 1, PIECE, W), vmem(HALVES, NX - 1, PIECE, W), vmem(HALVES, PIECE, W, kind=F32),
            vmem(HALVES, NZ - 1, OWN, W), vmem(HALVES, NZ - 1, OWN, W),
            pltpu.SemaphoreType.DMA((19,)), pltpu.SemaphoreType.DMA((COPIES,)), pltpu.SemaphoreType.DMA((COPIES,)),
        ],
        compiler_params=pltpu.CompilerParams(
            collective_id=0, has_side_effects=True, vmem_limit_bytes=52 * 2**20),
        name="boost",
    )(predictions, labels, feature_codes, leaf_index, sketch_weight)
    hist, values, updated = pl.pallas_call(
        store,
        out_shape=(
            jax.ShapeDtypeStruct((OWN, K), F32),
            jax.ShapeDtypeStruct((LEAVES, L), F32),
            jax.ShapeDtypeStruct((R, L), BF16),
        ),
        in_specs=[pl.BlockSpec(memory_space=pltpu.VMEM)] * 3,
        out_specs=[pl.BlockSpec(memory_space=pl.ANY)] * 3,
        scratch_shapes=[pltpu.SemaphoreType.DMA((NY + 2,))],
        compiler_params=pltpu.CompilerParams(vmem_limit_bytes=2**20),
        name="store",
    )(hist, values, updated)
    return hist.reshape(BINS // LEAVES, F, K), values, updated


def solution(mesh):
    return jax.shard_map(
        local,
        mesh=mesh,
        in_specs=(
            P("rows", "feat"),
            P("rows", "feat"),
            P("feat", "rows"),
            P("rows"),
            P("feat", None),
        ),
        out_specs=(P("rows", "feat", None), P(None, "feat"), P("rows", "feat")),
        check_vma=False,
    )
```
